32 devices in a mesh: space: 32 (over z, y, x, core), dp: 1.
Axes of the slice: x: 2, y: 2, z: 4, core: 2. Of those that a mesh axis runs over, the one named last changes fastest.
Arguments:
- activations: bfloat16 [1, 128, 16, 16, 128], P('dp', 'space'), may hold values from -100 to 100
- upstream: bfloat16 [1, 128, 16, 16, 128], P('dp', 'space'), may hold values from -100 to 100
- kernel_weight: bfloat16 [27, 128, 128], replicated, may hold values from -0.109375 to 0.109375
- patch_inverse: float32 [27, 128, 3456], P(None, 'space'), may hold values from -0.1 to 1.6, as said below
- output_inverse: float32 [128, 128], replicated, may hold values from -0.1 to 1.6, as said below
Outputs:
- activated: bfloat16 [1, 128, 16, 16, 128], P('dp', 'space')
- input_grad: bfloat16 [1, 128, 16, 16, 128], P('dp', 'space')
- patch_factor: float32 [128, 63, 128], P('space', None, 'dp')
- output_factor: float32 [128, 128], replicated
- precond_grad: float32 [27, 128, 128], P(None, 'space')
The draws below stay inside these ranges and needn't reach their ends.
Inputs may be any that keep to these rules, and one draw needn't show every extreme that they name: Symmetric as a 3456 x 3456 matrix whose row o * 128 + c is patch_inverse[o, c, :]. `output_inverse`: symmetric.
All inputs are finite; a program needn't handle non-finite values.
Results may differ from the reference program's by a relative error of at most 0.0015.
The reference program's roundings to bfloat16 on the way (of `slope`) count: a program that leaves them out, or rounds other values in their place, can miss the bound.
Values may be sent and summed in bfloat16 or wider, within the bound.
No kernel may reach another device: no remote copies, remote signals or barrier semaphores. Data moves between devices by JAX's collectives and lax.ppermute only.
A program may use at most 128 MiB of HBM per device.

```python
import math
import jax
import jax.numpy as jnp
from jax import lax

C = 128
TAPS = 27
LAGS = 63
CZ = 4
NY = 16
NX = 16
PATCH = 3456
VOLS = 1
NZ = 128
CELLS_ALL = 32768


def shared_field(key):
    field_shape = (VOLS, NZ, NY, NX, C)
    noise_field = jax.random.normal(jax.random.fold_in(key, 101), field_shape, jnp.float32)
    smooth = (noise_field + 0.6 * jnp.roll(noise_field, 1, 1) + 0.4 * jnp.roll(noise_field, 1, 2) + 0.4 * jnp.roll(noise_field, 1, 3)) / math.sqrt(1.68)
    mixing = jnp.eye(C, dtype=jnp.float32) + 0.4 * jax.random.normal(jax.random.fold_in(key, 102), (C, C), jnp.float32) / math.sqrt(C)
    mixed_field = jnp.dot(smooth.reshape(-1, C), mixing).reshape(field_shape)
    chan_scale = jnp.exp(jax.random.uniform(jax.random.fold_in(key, 103), (C,), jnp.float32, math.log(0.3), math.log(3.0)))
    depth_ramp = jnp.exp(0.55 * jnp.arange(NZ, dtype=jnp.float32) / NZ)
    slab_count = NZ // CZ
    slab_owner = jax.random.permutation(jax.random.fold_in(key, 104), slab_count)
    slab_of = jnp.arange(NZ) // CZ
    block_of = jnp.arange(C) // (C // slab_count)
    spike_gain = jnp.where(slab_owner[slab_of][:, None] == block_of[None, :], 3.0, 1.0)
    return mixed_field * chan_scale * depth_ramp[None, :, None, None, None] * spike_gain[None, :, None, None, :]


def draw_activations(key, part):
    return jnp.clip(shared_field(key), -100.0, 100.0).astype(jnp.bfloat16)


def draw_upstream(key, part):
    extra = jax.random.normal(jax.random.fold_in(key, 105), (VOLS, NZ, NY, NX, C), jnp.float32)
    return jnp.clip(0.3 * shared_field(key) + extra, -100.0, 100.0).astype(jnp.bfloat16)


def symmetric_inverse(key, order):
    reach = min(0.05, 0.6 / math.sqrt(order))
    entries = jax.random.uniform(jax.random.fold_in(key, 1), (order, order), jnp.float32, -reach, reach)
    diagonal = jax.random.uniform(jax.random.fold_in(key, 2), (order,), jnp.float32, 0.5, 1.45)
    return entries + entries.T + jnp.diag(diagonal)


def draw_patch_inverse(key, part):
    return symmetric_inverse(jax.random.fold_in(key, 201), PATCH).reshape(TAPS, C, PATCH)


def draw_output_inverse(key, part):
    return symmetric_inverse(jax.random.fold_in(key, 202), C)


def scatter_about(own_key, shape, width, most, held_as=jnp.bfloat16):
    return jnp.clip(width * jax.random.normal(own_key, shape, jnp.float32), -most, most).astype(held_as)


def setup_inputs(seed: int = 0) -> dict:
    arg_keys = jax.random.split(jax.random.key(seed), 6)
    return {
        "activations": draw_activations(jax.random.fold_in(arg_keys[5], 71), 0),
        "upstream": draw_upstream(jax.random.fold_in(arg_keys[5], 71), 0),
        "kernel_weight": scatter_about(arg_keys[2], (TAPS, C, C), PATCH ** -0.5, 0.109375),
        "patch_inverse": draw_patch_inverse(jax.random.fold_in(arg_keys[5], 71), 0),
        "output_inverse": draw_output_inverse(jax.random.fold_in(arg_keys[5], 71), 0),
    }


def tap_shift(offset):
    return (offset // 9 - 1, (offset // 3) % 3 - 1, offset % 3 - 1)


def lag_shift(lag):
    number = lag + 62
    return (number // 25 - 2, (number // 5) % 5 - 2, number % 5 - 2)


def rolled(field, displacement):
    return jnp.roll(field, (-displacement[0], -displacement[1], -displacement[2]), axis=(1, 2, 3))


def reference(activations, upstream, kernel_weight, patch_inverse, output_inverse):
    pre = jnp.zeros((CELLS_ALL, C), jnp.float32)
    for offset in range(TAPS):
        moved = rolled(activations, tap_shift(offset)).reshape(-1, C)
        pre = pre + jnp.dot(moved, kernel_weight[offset], preferred_element_type=jnp.float32)
    logistic = jax.nn.sigmoid(pre)
    activated = (pre * logistic).astype(jnp.bfloat16).reshape(activations.shape)
    slope = (upstream.reshape(-1, C).astype(jnp.float32) * logistic * (1.0 + pre * (1.0 - logistic))).astype(jnp.bfloat16)
    slope_field = slope.reshape(activations.shape)
    back = jnp.zeros((CELLS_ALL, C), jnp.float32)
    grads = []
    for offset in range(TAPS):
        displacement = tap_shift(offset)
        negated = (-displacement[0], -displacement[1], -displacement[2])
        slope_moved = rolled(slope_field, negated).reshape(-1, C)
        back = back + jnp.dot(slope_moved, kernel_weight[offset].T, preferred_element_type=jnp.float32)
        moved = rolled(activations, displacement).reshape(-1, C)
        grads.append(jnp.dot(moved.T, slope, preferred_element_type=jnp.float32))
    input_grad = back.astype(jnp.bfloat16).reshape(activations.shape)
    weight_grad = jnp.stack(grads, axis=0) / CELLS_ALL
    output_factor = jnp.dot(slope.T, slope, preferred_element_type=jnp.float32) / CELLS_ALL
    flat = activations.reshape(-1, C)
    blocks = []
    for lag in range(LAGS):
        moved = rolled(activations, lag_shift(lag)).reshape(-1, C)
        blocks.append(jnp.dot(flat.T, moved, preferred_element_type=jnp.float32))
    patch_factor = jnp.stack(blocks, axis=1) / CELLS_ALL
    left = jnp.dot(patch_inverse.reshape(PATCH, PATCH), weight_grad.reshape(PATCH, C), precision=lax.Precision.HIGHEST)
    precond_grad = jnp.dot(left, output_inverse, precision=lax.Precision.HIGHEST).reshape(TAPS, C, C)
    return activated, input_grad, patch_factor, output_factor, precond_grad
```

```python
import functools
import math

import jax
import jax.numpy as jnp
from jax import lax
from jax.experimental import pallas as pl
from jax.experimental.pallas import tpu as pltpu
from jax.sharding import PartitionSpec as P

F32 = jnp.float32
BF16 = jnp.bfloat16
TAPS = 27
SIDE = 3
LAGS = 63
GROUP = 8


def vmem():
    return pl.BlockSpec(memory_space=pltpu.VMEM)


def smem():
    return pl.BlockSpec(memory_space=pltpu.SMEM)


def lag_shift(lag):
    number = lag + 62
    return (number // 25 - 2, number // 5 % 5 - 2, number % 5 - 2)


def lag_blocks():
    blocks = []
    for lag in range(LAGS):
        dz, dy, dx = lag_shift(lag)
        key = (dz, dy, dx - dx % 2)
        if key not in blocks:
            blocks.append(key)
    return blocks


def call(kernel, outs, scratch, args, scalars=1, limit=None):
    return pl.pallas_call(
        kernel,
        out_shape=[jax.ShapeDtypeStruct(s, d) for s, d in outs],
        in_specs=[smem()] * scalars + [vmem()] * (len(args) - scalars),
        out_specs=[vmem()] * len(outs),
        scratch_shapes=[pltpu.VMEM(s, d) for s, d in scratch],
        compiler_params=pltpu.CompilerParams(vmem_limit_bytes=limit),
        name=kernel.__name__ if hasattr(kernel, "__name__") else kernel.func.__name__,
    )(*args)


def roll_x(rows, shift, ny, nx):
    cube = rows.reshape(ny, nx, rows.shape[-1])
    shift = shift % nx
    cube = jnp.concatenate([cube[:, nx - shift :], cube[:, : nx - shift]], axis=1)
    return cube.reshape(rows.shape)


def pad_planes(dst, own, low, high):
    depth, ny, nx, chans = own.shape
    plane = ny * nx
    for p in range(depth + 2):
        src = low[0] if p == 0 else high[0] if p == depth + 1 else own[p - 1]
        flat = src.reshape(plane, chans)
        dst[p, nx : nx + plane] = flat
        dst[p, :nx] = flat[plane - nx :]
        dst[p, nx + plane :] = flat[:nx]


def forward_kernel(scale, idx, act, low, high, up, w, actv, slope, keep, send, apad, wcat, s3, at, wg):
    depth, ny, nx, c = act.shape
    plane = ny * nx
    pad_planes(apad, act, low, high)
    for o in range(TAPS):
        q, x = divmod(o, SIDE)
        wcat[q * c : (q + 1) * c, x * c : (x + 1) * c] = w[o]
    for z in range(depth):
        lhs = jnp.concatenate(
            [apad[z + a, b * nx : b * nx + plane] for a in range(SIDE) for b in range(SIDE)], axis=1
        )
        zz = jnp.dot(lhs, wcat[...], preferred_element_type=F32)
        pre = (
            zz[:, c : 2 * c]
            + roll_x(zz[:, :c], 1, ny, nx)
            + roll_x(zz[:, 2 * c :], -1, ny, nx)
        )
        logistic = jax.nn.sigmoid(pre)
        actv[z] = (pre * logistic).astype(BF16).reshape(ny, nx, c)
        grad = (
            up[z].reshape(plane, c).astype(F32) * logistic * (1.0 + pre * (1.0 - logistic))
        ).astype(BF16)
        slope[z] = grad.reshape(ny, nx, c)
        wide = grad.astype(F32)
        rows = slice(z * plane, (z + 1) * plane)
        s3[rows, :c] = roll_x(wide, -1, ny, nx).astype(BF16)
        s3[rows, c : 2 * c] = grad
        s3[rows, 2 * c :] = roll_x(wide, 1, ny, nx).astype(BF16)
    for p in range(depth + 2):
        for b in range(SIDE):
            at[b, :, p * plane : (p + 1) * plane] = apad[p, b * nx : b * nx + plane].T
    for a in range(SIDE):
        for b in range(SIDE):
            lhs = at[b, :, a * plane : (a + depth) * plane]
            out = jnp.dot(lhs, s3[...], preferred_element_type=F32) * scale
            for x in range(SIDE):
                o = (a * SIDE + b) * SIDE + x
                wg[o * c : (o + 1) * c] = out[:, x * c : (x + 1) * c]
    middle = s3[:, c : 2 * c]
    wg[TAPS * c :] = jnp.dot(middle.T, middle, preferred_element_type=F32) * scale
    half = wg.shape[0] // 2
    core = idx[0] & 1
    keep[...] = wg[pl.ds(pl.multiple_of(core * half, 8), half)]
    send[...] = wg[pl.ds(pl.multiple_of((1 - core) * half, 8), half)]


def back_kernel(own, low, high, w, out, spad, wt):
    depth, ny, nx, c = own.shape
    plane = ny * nx
    pad_planes(spad, own, low, high)
    for o in range(TAPS):
        q, x = divmod(o, SIDE)
        wt[x * c : (x + 1) * c, q * c : (q + 1) * c] = w[o]
    for z in range(depth):
        lhs = jnp.concatenate(
            [
                spad[z + 2 - a, (2 - b) * nx : (2 - b) * nx + plane]
                for a in range(SIDE)
                for b in range(SIDE)
            ],
            axis=1,
        )
        zz = lax.dot_general(lhs, wt[...], (((1,), (1,)), ((), ())), preferred_element_type=F32)
        total = (
            zz[:, c : 2 * c]
            + roll_x(zz[:, :c], -1, ny, nx)
            + roll_x(zz[:, 2 * c :], 1, ny, nx)
        )
        out[z] = total.astype(BF16).reshape(ny, nx, c)


def split_kernel(idx, kept, got, *outs):
    quarters = len(outs)
    rows = outs[0].shape[0]
    here = (idx[0] // 2) % quarters
    for k in range(quarters):
        at = pl.ds(pl.multiple_of((here ^ k) * rows, 8), rows)
        outs[k][...] = kept[at] + got[at]


def layer_kernel(group, quarters, idx, *refs):
    parts, outs = refs[:quarters], refs[quarters:-1]
    total = refs[-1]
    value = parts[0][...]
    for part in parts[1:]:
        value = value + part[...]
    total[...] = value
    rows = outs[0].shape[0]
    here = idx[0] // group
    for k in range(len(outs)):
        outs[k][...] = total[pl.ds(pl.multiple_of((here ^ k) * rows, 8), rows)]


def lag_kernel(group, scale, own, idx, low, sel, *refs):
    slabs, rest = refs[:group], refs[group:]
    outs, (af, lhs, right, acc) = rest[:-4], rest[-4:]
    depth, ny, nx, c = slabs[0].shape
    plane = ny * nx
    cells = depth * plane
    count = sel.shape[0]
    blocks = lag_blocks()
    here = idx[0] & (group - 1)
    nt = (((1,), (1,)), ((), ()))
    af[:, : 2 * plane] = lax.dot_general(
        sel[...], low[...].reshape(2 * plane, c), nt, preferred_element_type=F32
    )
    for r in range(group):
        at = here ^ r
        flat = slabs[r][...].reshape(cells, c)
        af[:, pl.ds(pl.multiple_of(2 * plane + at * cells, 128), cells)] = lax.dot_general(
            sel[...], flat, nt, preferred_element_type=F32
        )
        rows = pl.ds(pl.multiple_of(at * cells, 16), cells)
        right[rows, :c] = flat
        right[rows, c:] = roll_x(flat.astype(F32), -1, depth * ny, nx).astype(BF16)
    column = lax.broadcasted_iota(jnp.int32, (count, plane), 1) % nx

    def fill(p, carry):
        base = af[:, pl.ds(pl.multiple_of(p * plane, 128), plane)]
        for dxb in (-2, 0, 2):
            moved = base
            if dxb > 0:
                moved = jnp.where(
                    column < dxb,
                    pltpu.roll(base, (dxb - nx) % plane, 1),
                    pltpu.roll(base, dxb, 1),
                )
            elif dxb < 0:
                moved = jnp.where(
                    column >= nx + dxb,
                    pltpu.roll(base, nx + dxb, 1),
                    pltpu.roll(base, dxb % plane, 1),
                )
            for dy in range(-2, 3):
                tile = (moved if dy == 0 else pltpu.roll(moved, (nx * dy) % plane, 1)).astype(BF16)
                for dz in range(3):
                    if (dz, dy, dxb) in blocks:
                        b = blocks.index((dz, dy, dxb))
                        lhs[b * count : (b + 1) * count, pl.ds(pl.multiple_of((p + dz) * plane, 128), plane)] = tile
        return carry

    lax.fori_loop(0, group * depth + 2, fill, 0)
    acc[...] = jnp.zeros_like(acc)

    def multiply(s, carry):
        left = lhs[:, pl.ds(pl.multiple_of(2 * plane + s * cells, 128), cells)]
        acc[...] += jnp.dot(
            left, right[pl.ds(pl.multiple_of(s * cells, 16), cells)], preferred_element_type=F32
        )
        return carry

    lax.fori_loop(0, group, multiply, 0)
    for out in outs:
        out[LAGS * own :] = jnp.zeros((out.shape[0] - LAGS * own, c), F32)
    for lag in range(LAGS):
        dz, dy, dx = lag_shift(lag)
        odd = dx % 2
        b = blocks.index((dz, dy, dx - odd))
        for k, out in enumerate(outs):
            start = b * count + k * own
            out[lag * own : (lag + 1) * own] = (
                acc[start : start + own, odd * c : (odd + 1) * c] * scale
            )


def factor_kernel(*refs):
    parts, out, total = refs[:-2], refs[-2], refs[-1]
    value = parts[0][...]
    for part in parts[1:]:
        value = value + part[...]
    total[...] = value
    own = out.shape[0]
    for j in range(own):
        out[j] = total[pl.ds(j, LAGS, stride=own)]


def halve_kernel(inverse, out, flat):
    taps, own, patch = inverse.shape
    rows = out.shape[0] // 2
    flat[taps * own :] = jnp.zeros((rows - taps * own, patch), F32)
    for o in range(taps):
        flat[o * own : (o + 1) * own] = inverse[o]
    value = flat[...]
    upper = value.astype(BF16)
    out[:rows] = upper
    out[rows:] = (value - upper.astype(F32)).astype(BF16)


def precond_kernel(group, layers, idx, halves, q, *refs):
    quarters = group // 2
    parts = refs[:group]
    out, factor, w = refs[group:]
    taps, own, c = out.shape
    patch = halves.shape[1]
    rows = parts[0].shape[0] // layers
    core = idx[0] & 1
    here = (idx[0] // 2) % quarters
    layer = idx[0] // group
    for r in range(group):
        k, other = divmod(r, 2)
        for m in range(layers):
            block = ((core ^ other) * quarters + (here ^ k)) * layers + (layer ^ m)
            w[pl.ds(pl.multiple_of(block * rows, 8), rows)] = parts[r][m * rows : (m + 1) * rows]
    factor[...] = w[patch:]
    value = w[:patch]
    upper = value.astype(BF16)
    both = jnp.concatenate([upper, (value - upper.astype(F32)).astype(BF16)], axis=1)
    product = jnp.dot(halves[...], both, preferred_element_type=F32)
    n = halves.shape[0] // 2
    left = (product[n:, :c] + product[:n, c:]) + product[n:, c:] + product[:n, :c]
    result = jnp.dot(left, q[...], precision=lax.Precision.HIGHEST, preferred_element_type=F32)
    for o in range(taps):
        out[o] = result[o * own : (o + 1) * own]


def per_device(activations, upstream, kernel_weight, patch_inverse, output_inverse):
    n = lax.axis_size("space")
    dp = lax.axis_size("dp")
    group = math.gcd(n, GROUP)
    quarters = group // 2
    layers = n // group
    _, depth, ny, nx, c = activations.shape
    plane = ny * nx
    cells = depth * plane
    own = patch_inverse.shape[1]
    patch = patch_inverse.shape[2]
    scale = 1.0 / float(cells * n * dp)
    me = lax.axis_index("space").astype(jnp.int32)
    idx = me.reshape(1)

    def flip(x, bits):
        return lax.ppermute(x, "space", [(i, i ^ bits) for i in range(n)])

    def shift(x, by):
        return lax.ppermute(x, "space", [(i, (i + by) % n) for i in range(n)])

    act = activations[0]
    up = upstream[0]
    low = shift(act[depth - 1 :], 1)
    high = shift(act[:1], -1)
    side = [act] + [flip(act, 2 * k) for k in range(1, quarters)]
    slabs = []
    for part in side:
        slabs += [part, flip(part, 1)]

    rows = (TAPS + 1) * c
    pad = (depth + 2, plane + 2 * nx, c)
    forward = functools.partial(forward_kernel, scale)
    actv, slope, keep, send = call(
        forward,
        [(act.shape, BF16), (act.shape, BF16), ((rows // 2, c), F32), ((rows // 2, c), F32)],
        [
            (pad, BF16),
            ((9 * c, 3 * c), BF16),
            ((cells, 3 * c), BF16),
            ((SIDE, c, (depth + 2) * plane), BF16),
            ((rows, c), F32),
        ],
        (idx, act, low, high, up, kernel_weight),
    )
    got = flip(send, 1)
    slope_low = shift(slope[depth - 1 :], 1)
    slope_high = shift(slope[:1], -1)
    piece = rows // group
    quarter = call(split_kernel, [((piece, c), F32)] * quarters, [], (idx, keep, got))
    quarter = [quarter[0]] + [flip(quarter[k], 2 * k) for k in range(1, quarters)]

    last = lax.select_n(
        (me % group) ^ (group - 1), *[slab[depth - 2 :] for slab in slabs]
    )
    below = shift(last, group)
    number = jnp.arange(layers * own, dtype=jnp.int32)
    layer = number // own ^ me // group
    channel = (layer * group + me % group) * own + number % own
    sel = (channel[:, None] == jnp.arange(c, dtype=jnp.int32)[None, :]).astype(BF16)
    count = layers * own
    nblocks = len(lag_blocks())
    lag_rows = -(-LAGS * own // 8) * 8
    lag = functools.partial(lag_kernel, group, scale, own)
    partial = call(
        lag,
        [((lag_rows, c), F32)] * layers,
        [
            ((count, (group * depth + 2) * plane), F32),
            ((nblocks * count, (group * depth + 4) * plane), BF16),
            ((group * cells, 2 * c), BF16),
            ((nblocks * count, 2 * c), F32),
        ],
        (idx, below, sel, *slabs),
        limit=50 << 20,
    )

    (input_grad,) = call(
        back_kernel,
        [(act.shape, BF16)],
        [(pad, BF16), ((3 * c, 9 * c), BF16)],
        (slope, slope_low, slope_high, kernel_weight),
        scalars=0,
    )

    thin = piece // layers
    layered = functools.partial(layer_kernel, group, quarters)
    pieces = call(
        layered, [((thin, c), F32)] * layers, [((piece, c), F32)], (idx, *quarter)
    )
    mine = pieces[0]
    for k in range(1, layers):
        mine = mine + flip(pieces[k], k * group)
    if dp > 1:
        mine = lax.psum(mine, "dp")
    column = jnp.concatenate([mine] + [flip(mine, k * group) for k in range(1, layers)], axis=0)
    whole = []
    for k in range(quarters):
        part = column if k == 0 else flip(column, 2 * k)
        whole += [part, flip(part, 1)]

    lag_parts = [partial[0]] + [flip(partial[k], k * group) for k in range(1, layers)]
    (patch_factor,) = call(
        factor_kernel, [((own, LAGS, c), F32)], [((lag_rows, c), F32)], tuple(lag_parts), scalars=0
    )
    if dp > 1:
        patch_factor = lax.psum_scatter(patch_factor, "dp", scatter_dimension=2, tiled=True)

    half_rows = -(-TAPS * own // 16) * 16
    (halves,) = call(
        halve_kernel, [((2 * half_rows, patch), BF16)], [((half_rows, patch), F32)], (patch_inverse,), scalars=0
    )
    precond = functools.partial(precond_kernel, group, layers)
    precond_grad, output_factor = call(
        precond,
        [((TAPS, own, c), F32), ((c, c), F32)],
        [((rows, c), F32)],
        (idx, halves, output_inverse, *whole),
    )
    return (actv[None], input_grad[None], patch_factor, output_factor, precond_grad)


def solution(mesh):
    return jax.shard_map(
        per_device,
        mesh=mesh,
        in_specs=(
            P("dp", "space", None, None, None),
            P("dp", "space", None, None, None),
            P(),
            P(None, "space", None),
            P(),
        ),
        out_specs=(
            P("dp", "space", None, None, None),
            P("dp", "space", None, None, None),
            P("space", None, "dp"),
            P(),
            P(None, "space", None),
        ),
        check_vma=False,
    )
```
